256 devices in a mesh: row: 32 (over z, y), col: 8 (over x, core).
Axes of the slice: x: 4, y: 4, z: 8, core: 2. Of those that a mesh axis runs over, the one named last changes fastest.
Arguments:
- right_sides: bfloat16 [128, 8, 384, 256], P('row', 'col'), may hold values from -120 to 120
- stiff_diag: bfloat16 [128, 8, 384, 384], P('row', 'col'), may hold values from -0.85 to 7.85
- stiff_upper: bfloat16 [128, 8, 384, 384], P('row', 'col'), may hold values from -0.635 to 0.635
- local_diag: bfloat16 [192, 8, 384, 384], P('row', 'col'), may hold values from -0.089 to 0.79
- local_upper: bfloat16 [160, 8, 384, 384], P('row', 'col'), may hold values from -0.034 to 0.034
- coarse_basis: bfloat16 [32, 8, 6, 1536], P('row', 'col'), may hold values from -0.21875 to 0.21875
- coarse_factor: bfloat16 [1536, 1536], replicated, may hold values from -0.15625 to 0.15625
Outputs:
- solution: float32 [128, 8, 384, 256], P('row', 'col')
The draws below stay inside these ranges and needn't reach their ends.
All inputs are finite; a program needn't handle non-finite values.
Results may differ from the reference program's by a relative error of at most 0.0018.
Values may be sent and summed in bfloat16 or wider, within the bound.
A program may use at most 64 MiB of HBM per device.

```python
import jax
import jax.numpy as jnp
from jax import lax

BS = 384
NB = 4
RHS = 256
NCB = 6
ITERS = 2
SUB_ROWS = 32
SUB_COLS = 8
LAYERS = 128
EXT_ROWS = 192
UPPER_ROWS = 160
NCO = 1536


def permuted_part(key, count, bound):
    key_perm, key_coef = jax.random.split(key)
    leading = (count, SUB_COLS)
    ordered = jnp.broadcast_to(jnp.arange(BS, dtype=jnp.int32), leading + (BS,))
    shuffled = jax.random.permutation(key_perm, ordered, axis=2, independent=True)
    weights = jax.random.uniform(key_coef, leading + (BS, 1), jnp.float32, -bound, bound)
    col_ids = lax.broadcasted_iota(jnp.int32, leading + (BS, BS), 3)
    return jnp.where(col_ids == shuffled[..., None], weights, 0.0)


def dense_part(key, count, bound):
    return jax.random.uniform(key, (count, SUB_COLS, BS, BS), jnp.float32, -bound, bound)


def symmetric_block(key, count, diag_low, diag_high, perm_bound, dense_bound):
    key_perm = jax.random.fold_in(key, 11)
    key_dense = jax.random.fold_in(key, 12)
    key_diag = jax.random.fold_in(key, 13)
    scattered = permuted_part(key_perm, count, perm_bound)
    noise = dense_part(key_dense, count, dense_bound)
    row_ids = lax.broadcasted_iota(jnp.int32, (count, SUB_COLS, BS, BS), 2)
    col_ids = lax.broadcasted_iota(jnp.int32, (count, SUB_COLS, BS, BS), 3)
    mirrored = jnp.where(row_ids <= col_ids, noise, jnp.swapaxes(noise, 2, 3))
    diag_vals = jax.random.uniform(key_diag, (count, SUB_COLS, BS, 1), jnp.float32, diag_low, diag_high)
    return mirrored + scattered + jnp.swapaxes(scattered, 2, 3) + jnp.where(row_ids == col_ids, diag_vals, 0.0)


def draw_right_sides(key, part):
    key_values = jax.random.fold_in(key, 21)
    key_scale = jax.random.fold_in(key, 22)
    full_shape = (LAYERS, SUB_COLS, BS, RHS)
    layer_pos = lax.broadcasted_iota(jnp.float32, full_shape, 0)
    rising = jnp.exp(jnp.log(3.0) * layer_pos / max(LAYERS - 1, 1))
    spread = jnp.exp(jax.random.uniform(key_scale, (LAYERS, SUB_COLS, BS, 1), jnp.float32, 0.0, jnp.log(10.0)))
    baseline = jnp.clip(jax.random.normal(key_values, full_shape, jnp.float32), -4.0, 4.0)
    return (baseline * spread * rising).astype(jnp.bfloat16)


def draw_stiff_diag(key, part):
    return symmetric_block(jax.random.fold_in(key, 31), LAYERS, 5.5, 7.0, 0.4, 0.05).astype(jnp.bfloat16)


def draw_stiff_upper(key, part):
    scattered = permuted_part(jax.random.fold_in(key, 41), LAYERS, 0.6)
    return (scattered + dense_part(jax.random.fold_in(key, 42), LAYERS, 0.035)).astype(jnp.bfloat16)


def draw_local_diag(key, part):
    return symmetric_block(jax.random.fold_in(key, 51), EXT_ROWS, 0.55, 0.7, 0.04, 0.0087).astype(jnp.bfloat16)


def draw_local_upper(key, part):
    scattered = permuted_part(jax.random.fold_in(key, 61), UPPER_ROWS, 0.03)
    return (scattered + dense_part(jax.random.fold_in(key, 62), UPPER_ROWS, 0.0035)).astype(jnp.bfloat16)


def block_levels(stream_key, extent, shards, low, largest):
    gain, own = 1.0, jax.random.fold_in(stream_key, 6)
    for axis_at, parts in shards:
        draws = jnp.exp(jax.random.uniform(jax.random.fold_in(own, axis_at), (parts,), jnp.float32, low / len(shards), largest / len(shards)))
        gain = gain * jnp.repeat(draws, extent[axis_at] // parts).reshape([-1 if axis == axis_at else 1 for axis in range(len(extent))])
    return gain


def bell_draw(stream_key, dims, scale, reach, shards=(), kind=jnp.bfloat16):
    values = scale * jax.random.normal(stream_key, dims, jnp.float32)
    if shards:
        values = values * block_levels(stream_key, dims, shards, -0.22, 0.18)
    return jnp.clip(values, -reach, reach).astype(kind)


def setup_inputs(seed: int = 0) -> dict:
    keys = jax.random.split(jax.random.key(seed), 8)
    right_sides = draw_right_sides(jax.random.fold_in(keys[7], 71), 0)
    stiff_diag = draw_stiff_diag(jax.random.fold_in(keys[7], 71), 0)
    stiff_upper = draw_stiff_upper(jax.random.fold_in(keys[7], 71), 0)
    local_diag = draw_local_diag(jax.random.fold_in(keys[7], 71), 0)
    local_upper = draw_local_upper(jax.random.fold_in(keys[7], 71), 0)
    coarse_basis = bell_draw(keys[5], (SUB_ROWS, SUB_COLS, NCB, NB * BS), (NB * BS // 2) ** -0.5, 0.21875, ((0, 32), (1, 8)))
    coarse_factor = bell_draw(keys[6], (NCO, NCO), NCO ** -0.5, 0.15625)
    return {"right_sides": right_sides, "stiff_diag": stiff_diag, "stiff_upper": stiff_upper, "local_diag": local_diag, "local_upper": local_upper, "coarse_basis": coarse_basis, "coarse_factor": coarse_factor}


def rounded(values):
    return lax.optimization_barrier(values.astype(jnp.bfloat16))


def multiply(blocks, vectors):
    return jnp.einsum("...ij,...jr->...ir", blocks.astype(jnp.float32), vectors.astype(jnp.float32))


def multiply_transposed(blocks, vectors):
    return jnp.einsum("...ji,...jr->...ir", blocks.astype(jnp.float32), vectors.astype(jnp.float32))


def column_slice(array, column):
    return lax.dynamic_index_in_dim(array, column, 1, keepdims=False)


def per_column(function):
    outputs = lax.map(function, jnp.arange(SUB_COLS, dtype=jnp.int32))
    return jnp.moveaxis(outputs, 0, 1)


def operate(vector, stiff_diag, stiff_upper):
    vec_bf = rounded(vector)

    def one_column(column):
        layers = column_slice(vec_bf, column)
        s_diag = column_slice(stiff_diag, column)
        s_upper = column_slice(stiff_upper, column)
        zero_layer = jnp.zeros((1,) + layers.shape[1:], jnp.float32)
        from_above = jnp.concatenate([multiply(s_upper[:-1], layers[1:]), zero_layer], axis=0)
        from_below = jnp.concatenate([zero_layer, multiply_transposed(s_upper[:-1], layers[:-1])], axis=0)
        return multiply(s_diag, layers) + from_above + from_below

    return per_column(one_column)


def local_solve(res_bf, local_diag, local_upper):
    def one_column(column):
        layers = column_slice(res_bf, column)
        diag_blocks = column_slice(local_diag, column).reshape(SUB_ROWS, NB + 2, BS, BS)
        upper_blocks = column_slice(local_upper, column).reshape(SUB_ROWS, NB + 1, BS, BS)
        padded = jnp.pad(layers, ((1, 1), (0, 0), (0, 0)))
        window_ids = jnp.arange(SUB_ROWS, dtype=jnp.int32)[:, None] * NB + jnp.arange(NB + 2, dtype=jnp.int32)[None, :]
        extended = padded[window_ids]
        zero_layer = jnp.zeros((SUB_ROWS, 1, BS, RHS), jnp.float32)
        solved = multiply(diag_blocks, extended)
        solved = solved + jnp.concatenate([multiply(upper_blocks, extended[:, 1:]), zero_layer], axis=1)
        solved = solved + jnp.concatenate([zero_layer, multiply_transposed(upper_blocks, extended[:, :-1])], axis=1)
        assembled = jnp.zeros(padded.shape, jnp.float32).at[window_ids].add(solved)
        return assembled[1:-1]

    return per_column(one_column)


def coarse_correction(res_bf, coarse_basis, coarse_factor):
    grouped = res_bf.reshape(SUB_ROWS, NB, SUB_COLS, BS, RHS).transpose(0, 2, 1, 3, 4)
    grouped = grouped.reshape(SUB_ROWS, SUB_COLS, NB * BS, RHS)
    coarse_rhs = jnp.einsum("abkn,abnr->abkr", coarse_basis.astype(jnp.float32), grouped.astype(jnp.float32))
    rhs_bf = coarse_rhs.reshape(NCO, RHS).astype(jnp.bfloat16)
    solved = jnp.dot(coarse_factor, rhs_bf, preferred_element_type=jnp.float32)
    coarse_sol = jnp.dot(coarse_factor.T, solved.astype(jnp.bfloat16), preferred_element_type=jnp.float32)
    sol_bf = rounded(coarse_sol).reshape(SUB_ROWS, SUB_COLS, NCB, RHS)
    spread = jnp.einsum("abkn,abkr->abnr", coarse_basis.astype(jnp.float32), sol_bf.astype(jnp.float32))
    spread = spread.reshape(SUB_ROWS, SUB_COLS, NB, BS, RHS).transpose(0, 2, 1, 3, 4)
    return spread.reshape(LAYERS, SUB_COLS, BS, RHS)


def precondition(residual, local_diag, local_upper, coarse_basis, coarse_factor):
    res_bf = rounded(residual)
    local_part = local_solve(res_bf, local_diag, local_upper)
    return local_part + coarse_correction(res_bf, coarse_basis, coarse_factor)


def reference(right_sides, stiff_diag, stiff_upper, local_diag, local_upper, coarse_basis, coarse_factor):
    residual = right_sides.astype(jnp.float32)
    solution = jnp.zeros_like(residual)
    direction = jnp.zeros_like(residual)
    rho_before = jnp.ones((RHS,), jnp.float32)
    for iteration in range(ITERS):
        precond = precondition(residual, local_diag, local_upper, coarse_basis, coarse_factor)
        rho_now = jnp.sum(residual * precond, axis=(0, 1, 2))
        if iteration == 0:
            direction = precond
        else:
            direction = precond + (rho_now / rho_before) * direction
        image_vec = operate(direction, stiff_diag, stiff_upper)
        step_len = rho_now / jnp.sum(direction * image_vec, axis=(0, 1, 2))
        solution = solution + step_len * direction
        residual = residual - step_len * image_vec
        rho_before = rho_now
    return solution
```

```python
import functools

import jax
import jax.numpy as jnp
from jax import lax
from jax.experimental import pallas as pl
from jax.experimental.pallas import tpu as pltpu
from jax.sharding import Mesh
from jax.sharding import PartitionSpec as P

MESH = pl.DeviceIdType.MESH
F32 = jnp.float32
BF = jnp.bfloat16


def mm(left, right):
    return jnp.dot(left, right, preferred_element_type=F32)


def stacked(ref, start, count):
    _, rows, cols = ref.shape
    return ref[pl.ds(start, count)].reshape(count * rows, cols)


def kernel(sizes, *refs):
    nz, ny, nx, nk = sizes
    (b_hbm, sd_hbm, su_hbm, ld_hbm, lu_hbm, cb_hbm, f_hbm, x_ref, *scratch) = refs
    (
        lm, sm, sut, cb, fac, fsel, sel, kk,
        ev0, ev1, pv, pv1, q0, w0, q1,
        y_dn, y_up, yr_dn, yr_up, t_up, tr, ub, cx, cxr_up, cxr_dn,
        gz, ups, upr, sums, red_c, red_y, red_z,
        load_sem, halo_send, halo_recv, gy_send, gy_recv, gzs_send, gzs_recv,
        u_send, u_recv, rc_send, rc_recv, ry_send, ry_recv, rz_send, rz_recv,
    ) = scratch
    nb = b_hbm.shape[0]
    bs, nr = b_hbm.shape[1:]
    ncb = cb_hbm.shape[0]
    nco = f_hbm.shape[0]
    half = nr // 2
    nrow, ncol = nz * ny, nx * nk
    z, y, x, k = (lax.axis_index(name) for name in ("z", "y", "x", "k"))
    row, col = z * ny + y, x * nk + k
    has_dn, has_up = row > 0, row < nrow - 1

    def row_device(index):
        return {"z": index // ny, "y": lax.rem(index, ny)}

    up_dev = row_device(lax.rem(row + 1, nrow))
    dn_dev = row_device(lax.rem(row + nrow - 1, nrow))

    def col_device(step):
        index = lax.rem(col + step, ncol)
        return {"x": index // nk, "k": lax.rem(index, nk)}

    def y_device(step):
        return {"y": lax.rem(y + step, ny)}

    def z_device(step):
        return {"z": lax.rem(z + step, nz)}

    loads = [
        pltpu.make_async_copy(b_hbm, ev0.at[pl.ds(1, nb)], load_sem.at[0]),
        pltpu.make_async_copy(cb_hbm, cb, load_sem.at[1]),
        pltpu.make_async_copy(lu_hbm, lm.at[pl.ds(0, nb + 1), :, pl.ds(2 * bs, bs)], load_sem.at[2]),
        pltpu.make_async_copy(ld_hbm, lm.at[:, :, pl.ds(bs, bs)], load_sem.at[3]),
        pltpu.make_async_copy(f_hbm, fac, load_sem.at[4]),
        pltpu.make_async_copy(su_hbm, sm.at[:, :, pl.ds(2 * bs, bs)], load_sem.at[5]),
        pltpu.make_async_copy(sd_hbm, sm.at[:, :, pl.ds(bs, bs)], load_sem.at[6]),
    ]
    for load in loads:
        load.start()

    barrier = pltpu.get_barrier_semaphore()
    peers = [up_dev, dn_dev]
    peers += [y_device(s) for s in range(1, ny)]
    peers += [col_device(s) for s in range(1, ncol)]
    peers += [z_device(s) for s in range(1, nz)]
    for peer in peers:
        pl.semaphore_signal(barrier, inc=1, device_id=peer, device_id_type=MESH)

    @pl.when(row == 0)
    def _():
        ev0[0] = jnp.zeros((bs, nr), BF)
        ev1[0] = jnp.zeros((bs, nr), BF)
        yr_dn[...] = jnp.zeros_like(yr_dn)
        tr[...] = jnp.zeros_like(tr)
        cxr_dn[...] = jnp.zeros_like(cxr_dn)

    @pl.when(row == nrow - 1)
    def _():
        ev0[nb + 1] = jnp.zeros((bs, nr), BF)
        ev1[nb + 1] = jnp.zeros((bs, nr), BF)
        pv[nb] = jnp.zeros((bs, nr), BF)
        yr_up[...] = jnp.zeros_like(yr_up)
        cxr_up[...] = jnp.zeros_like(cxr_up)

    rows_of = lax.broadcasted_iota(jnp.int32, sel.shape, 0)
    slots = lax.broadcasted_iota(jnp.int32, sel.shape, 1)
    slot, j = slots // 8, slots % 8
    owner = jnp.where(slot < nrow, slot * ncol + col, row * ncol + (slot - nrow))
    wanted = jnp.where(j < ncb, owner * ncb + j, -1)
    sel[...] = jnp.where(rows_of == wanted, 1.0, 0.0).astype(BF)

    loads[0].wait()
    pl.semaphore_wait(barrier, len(peers))

    def to_up(index, src, dst):
        return pltpu.make_async_remote_copy(
            src_ref=src, dst_ref=dst, send_sem=halo_send.at[index], recv_sem=halo_recv.at[index],
            device_id=up_dev, device_id_type=MESH,
        )

    def to_dn(index, src, dst):
        return pltpu.make_async_remote_copy(
            src_ref=src, dst_ref=dst, send_sem=halo_send.at[index], recv_sem=halo_recv.at[index],
            device_id=dn_dev, device_id_type=MESH,
        )

    halo = [
        (to_up(0, ev0.at[nb], ev0.at[0]), to_dn(1, ev0.at[1], ev0.at[nb + 1])),
        (to_up(2, y_up.at[0], yr_dn.at[0]), to_dn(3, y_dn.at[0], yr_up.at[0])),
        (to_up(4, t_up, tr), to_dn(5, pv.at[0], pv.at[nb])),
        (to_up(6, ev1.at[nb], ev1.at[0]), to_dn(7, ev1.at[1], ev1.at[nb + 1])),
        (to_up(8, y_up.at[1], yr_dn.at[1]), to_dn(9, y_dn.at[1], yr_up.at[1])),
        (to_up(10, cx.at[0], cxr_dn), to_dn(11, cx.at[1], cxr_up)),
    ]

    def send_up(phase):
        pl.when(has_up)(lambda: halo[phase][0].start())

    def send_dn(phase):
        pl.when(has_dn)(lambda: halo[phase][1].start())

    def receive(phase):
        pl.when(has_dn)(lambda: halo[phase][0].wait_recv())
        pl.when(has_up)(lambda: halo[phase][1].wait_recv())

    send_up(0)
    send_dn(0)

    def y_copies(it):
        here = gz.at[it, z, pl.ds(pl.multiple_of(y * 16, 16), 16)]
        return [
            pltpu.make_async_remote_copy(
                src_ref=here, dst_ref=here, send_sem=gy_send.at[it, s], recv_sem=gy_recv.at[it, s],
                device_id=y_device(s), device_id_type=MESH,
            )
            for s in range(1, ny)
        ]

    def z_copies(it):
        here = gz.at[it, z]
        return [
            pltpu.make_async_remote_copy(
                src_ref=here, dst_ref=here, send_sem=gzs_send.at[it, s], recv_sem=gzs_recv.at[it, s],
                device_id=z_device(s), device_id_type=MESH,
            )
            for s in range(1, nz)
        ]

    def u_copies(it):
        copies = []
        for s in range(1, ncol):
            target = lax.rem(col + s, ncol)
            copies.append(
                pltpu.make_async_remote_copy(
                    src_ref=ups.at[it, target], dst_ref=upr.at[it, s],
                    send_sem=u_send.at[it, s], recv_sem=u_recv.at[it, s],
                    device_id=col_device(s), device_id_type=MESH,
                )
            )
        return copies

    gy = [y_copies(it) for it in range(2)]
    gzc = [z_copies(it) for it in range(2)]
    uc = [u_copies(it) for it in range(2)]

    def coarse_begin(it, vec):
        g = mm(cb[...], stacked(vec, 1, nb))
        g = jnp.concatenate([g, jnp.zeros((8 - ncb, nr), F32)], axis=0)
        packed = jnp.concatenate([g[:, :half], g[:, half:]], axis=0).astype(BF)
        gz[it, z, pl.ds(pl.multiple_of(y * 16, 16), 16)] = packed
        for copy in gy[it]:
            copy.start()

    def coarse_spread_rows(it):
        for copy in gy[it]:
            copy.wait_recv()
        for copy in gzc[it]:
            copy.start()

    def coarse_solve(it):
        for copy in gzc[it]:
            copy.wait_recv()
        got = gz[it].astype(F32).reshape(nrow, 16, half)
        sides = [got[:, 8 * h : 8 * h + 8].reshape(nrow * 8, half) for h in range(2)]
        g = jnp.concatenate(sides, axis=1).astype(BF)
        u = mm(kk[0], g) + mm(kk[1], g)
        ups[it] = u.reshape(ncol, 8, nr)
        for copy in uc[it]:
            copy.start()

    def coarse_end(it):
        for copy in uc[it]:
            copy.wait_recv()
        u = ups[it, pl.ds(col, 1)].reshape(8, nr)
        for s in range(1, ncol):
            u = u + upr[it, s]
        return u[:ncb].astype(BF)

    def spread(u, layer):
        return lax.dot_general(
            cb[:, pl.ds(pl.multiple_of(layer * bs, bs), bs)], u, (((0,), (0,)), ((), ())),
            preferred_element_type=F32,
        )

    loads[1].wait()
    coarse_begin(0, ev0)

    loads[2].wait()

    @pl.loop(0, nb + 1)
    def _(i):
        lm[i + 1, :, pl.ds(0, bs)] = lm[i, :, pl.ds(2 * bs, bs)].T

    coarse_spread_rows(0)

    loads[3].wait()

    def local_middle(vec, out):
        @pl.loop(2, nb)
        def _(i):
            out[i - 1] = mm(lm[i], stacked(vec, i - 1, 3))

    def local_edges(it, vec, out):
        receive(3 * it)
        y_dn[it] = mm(lm[0, :, pl.ds(bs, 2 * bs)], stacked(vec, 0, 2)).astype(BF)
        send_dn(3 * it + 1)
        y_up[it] = mm(lm[nb + 1, :, pl.ds(0, 2 * bs)], stacked(vec, nb, 2)).astype(BF)
        send_up(3 * it + 1)

        @pl.loop(0, 2)
        def _(e):
            i = 1 + e * (nb - 1)
            out[i - 1] = mm(lm[i], stacked(vec, i - 1, 3))

    local_middle(ev0, q0)
    local_edges(0, ev0, q0)

    loads[4].wait()

    @pl.loop(0, nco // 256)
    def _(i):
        at = pl.ds(pl.multiple_of(i * 256, 256), 256)
        fsel[at, :] = mm(fac[at, :], sel[...]).astype(BF)

    split = nrow * 8
    kmat = lax.dot_general(
        fsel[:, split:], fsel[:, :split], (((0,), (0,)), ((), ())), preferred_element_type=F32
    )
    kk[0] = kmat.astype(BF)
    kk[1] = (kmat - kmat.astype(BF).astype(F32)).astype(BF)
    coarse_solve(0)

    loads[5].wait()

    @pl.loop(0, nb)
    def _(i):
        sut[i] = sm[i, :, pl.ds(2 * bs, bs)].T

    @pl.loop(1, nb)
    def _(i):
        sm[i, :, pl.ds(0, bs)] = sut[i - 1]

    loads[6].wait()

    def finish(it, out, u, vec):
        receive(3 * it + 1)
        out[0] += yr_dn[it].astype(F32)
        out[nb - 1] += yr_up[it].astype(F32)

        @pl.loop(0, nb)
        def _(i):
            total = out[i] + spread(u, i)
            out[i] = total
            vec[i] = total.astype(BF)

    finish(0, q0, coarse_end(0), pv)
    send_dn(2)
    t_up[...] = mm(sut[nb - 1], pv[nb - 1]).astype(BF)
    send_up(2)

    def stiff_inside(vec, store):
        store(0, mm(sm[0, :, pl.ds(bs, 2 * bs)], stacked(vec, 0, 2)))
        for i in range(1, nb - 1):
            store(i, mm(sm[i], stacked(vec, i - 1, 3)))
        store(nb - 1, mm(sm[nb - 1, :, pl.ds(0, 2 * bs)], stacked(vec, nb - 2, 2)))

    def store_w0(i, value):
        w0[i] = value

    stiff_inside(pv, store_w0)
    receive(2)
    ub[...] = mm(sm[nb - 1, :, pl.ds(2 * bs, bs)], pv[nb])
    w0[0] += tr[...].astype(F32)
    w0[nb - 1] += ub[...]
    ev1[1] = w0[0].astype(BF)
    send_dn(3)
    ev1[nb] = w0[nb - 1].astype(BF)
    send_up(3)
    for i in range(1, nb - 1):
        ev1[1 + i] = w0[i].astype(BF)
    coarse_begin(1, ev1)

    def columns(value):
        return jnp.sum(value, axis=0, keepdims=True)

    s1 = jnp.zeros((1, nr), F32)
    s2 = jnp.zeros((1, nr), F32)
    for i in range(nb):
        s1 = s1 + columns(ev0[1 + i].astype(F32) * q0[i])
        s2 = s2 + columns(w0[i] * q0[i])

    coarse_spread_rows(1)
    local_middle(ev1, q1)
    local_edges(1, ev1, q1)
    coarse_solve(1)
    finish(1, q1, coarse_end(1), pv1)
    cx[1] = pv1[0, :, pl.ds(0, half)]
    send_dn(5)
    cx[0] = mm(sut[nb - 1], pv1[nb - 1, :, pl.ds(half, half)]).astype(BF)
    send_up(5)

    s3 = jnp.zeros((1, nr), F32)
    s4 = jnp.zeros((1, nr), F32)
    for i in range(nb):
        s3 = s3 + columns(ev0[1 + i].astype(F32) * q1[i])
        s4 = s4 + columns(w0[i] * q1[i])
    s5 = columns(tr[...].astype(F32) * q1[0]) + columns(ub[...] * q1[nb - 1])
    mixed = []

    def add_dots(i, value):
        mixed.append((columns(q0[i] * value), columns(q1[i] * value)))

    stiff_inside(pv1, add_dots)
    s5 = s5 + sum(pair[0] for pair in mixed)
    s6 = sum(pair[1] for pair in mixed)
    receive(5)
    from_up = mm(sm[nb - 1, :, pl.ds(2 * bs, bs)], cxr_up[...])
    cross_up = columns(from_up * q1[nb - 1, :, pl.ds(0, half)])
    cross_dn = columns(cxr_dn[...].astype(F32) * q1[0, :, pl.ds(half, half)])
    s6 = s6 + 2.0 * jnp.concatenate([cross_up, cross_dn], axis=1)

    sums[0] = jnp.concatenate([s1, s2, s3, s4, s5, s6, jnp.zeros((2, nr), F32)], axis=0)

    def reduce_stage(stage, buf, device, count, send, recv):
        copies = [
            pltpu.make_async_remote_copy(
                src_ref=sums.at[stage], dst_ref=buf.at[s], send_sem=send.at[s], recv_sem=recv.at[s],
                device_id=device(s), device_id_type=MESH,
            )
            for s in range(1, count)
        ]
        for copy in copies:
            copy.start()
        total = sums[stage]
        for s, copy in enumerate(copies, 1):
            copy.wait_recv()
            total = total + buf[s]
        return copies, total

    sent_c, total = reduce_stage(0, red_c, col_device, ncol, rc_send, rc_recv)
    sums[1] = total
    sent_y, total = reduce_stage(1, red_y, y_device, ny, ry_send, ry_recv)
    sums[2] = total
    sent_z, total = reduce_stage(2, red_z, z_device, nz, rz_send, rz_recv)

    d = [total[i : i + 1] for i in range(6)]
    alpha = d[0] / d[1]
    rho = d[0] - alpha * (d[2] + d[1]) + alpha * alpha * d[3]
    grow = 1.0 + rho / d[0]
    denom = grow * grow * d[1] - grow * alpha * (d[4] + d[3]) + alpha * alpha * d[5]
    step = rho / denom
    c0 = jnp.broadcast_to(alpha + step * grow, (bs, nr))
    c1 = jnp.broadcast_to(alpha * step, (bs, nr))
    for i in range(nb):
        x_ref[i] = c0 * q0[i] - c1 * q1[i]

    for copy in sent_c + sent_y + sent_z + gy[0] + gy[1] + gzc[0] + gzc[1] + uc[0] + uc[1]:
        copy.wait_send()
    for up, dn in halo:
        pl.when(has_up)(lambda up=up: up.wait_send())
        pl.when(has_dn)(lambda dn=dn: dn.wait_send())


def on_device(sizes, b, sd, su, ld, lu, cb, fac):
    nz, ny, nx, nk = sizes
    b, sd, su, ld, lu = (a[:, 0] for a in (b, sd, su, ld, lu))
    cb = cb[0, 0]
    nb, bs, nr = b.shape
    ncb = cb.shape[0]
    nco = fac.shape[0]
    nrow, ncol = nz * ny, nx * nk
    half = nr // 2
    nsel = 8 * (nrow + ncol)
    dma = pltpu.SemaphoreType.DMA
    vm = pltpu.VMEM
    scratch = [
        vm((nb + 2, bs, 3 * bs), BF),
        vm((nb, bs, 3 * bs), BF),
        vm((nb, bs, bs), BF),
        vm((ncb, nb * bs), BF),
        vm((nco, nco), BF),
        vm((nco, nsel), BF),
        vm((nco, nsel), BF),
        vm((2, 8 * ncol, 8 * nrow), BF),
        vm((nb + 2, bs, nr), BF),
        vm((nb + 2, bs, nr), BF),
        vm((nb + 1, bs, nr), BF),
        vm((nb, bs, nr), BF),
        vm((nb, bs, nr), F32),
        vm((nb, bs, nr), F32),
        vm((nb, bs, nr), F32),
        vm((2, bs, nr), BF),
        vm((2, bs, nr), BF),
        vm((2, bs, nr), BF),
        vm((2, bs, nr), BF),
        vm((bs, nr), BF),
        vm((bs, nr), BF),
        vm((bs, nr), F32),
        vm((2, bs, half), BF),
        vm((bs, half), BF),
        vm((bs, half), BF),
        vm((2, nz, ny * 16, half), BF),
        vm((2, ncol, 8, nr), F32),
        vm((2, ncol, 8, nr), F32),
        vm((3, 8, nr), F32),
        vm((ncol, 8, nr), F32),
        vm((ny, 8, nr), F32),
        vm((nz, 8, nr), F32),
        dma((7,)),
        dma((12,)),
        dma((12,)),
        dma((2, ny)),
        dma((2, ny)),
        dma((2, nz)),
        dma((2, nz)),
        dma((2, ncol)),
        dma((2, ncol)),
        dma((ncol,)),
        dma((ncol,)),
        dma((ny,)),
        dma((ny,)),
        dma((nz,)),
        dma((nz,)),
    ]
    out = pl.pallas_call(
        functools.partial(kernel, sizes),
        out_shape=jax.ShapeDtypeStruct((nb, bs, nr), F32),
        in_specs=[pl.BlockSpec(memory_space=pl.ANY)] * 7,
        out_specs=pl.BlockSpec(memory_space=pltpu.VMEM),
        scratch_shapes=scratch,
        compiler_params=pltpu.CompilerParams(
            collective_id=0, has_side_effects=True, vmem_limit_bytes=60 * 1024 * 1024
        ),
        name="schwarz_pcg",
    )(b, sd, su, ld, lu, cb, fac)
    return out[:, None]


def solution(mesh):
    sizes = (8, 4, 4, 2)
    if mesh.devices.size != 256:
        sizes = (2, 2, 2, 2)
    split = Mesh(mesh.devices.reshape(sizes), ("z", "y", "x", "k"))
    row, col = ("z", "y"), ("x", "k")
    spec = P(row, col, None, None)
    return jax.shard_map(
        functools.partial(on_device, sizes),
        mesh=split,
        in_specs=(spec,) * 6 + (P(),),
        out_specs=spec,
        check_vma=False,
    )
```

```python
import functools

import jax
import jax.numpy as jnp
from jax import lax
from jax.experimental import pallas as pl
from jax.experimental.pallas import tpu as pltpu
from jax.sharding import Mesh
from jax.sharding import PartitionSpec as P

MESH = pl.DeviceIdType.MESH
F32 = jnp.float32
BF = jnp.bfloat16


def mm(left, right):
    return jnp.dot(left, right, preferred_element_type=F32)


def stacked(ref, start, count):
    _, rows, cols = ref.shape
    return ref[pl.ds(start, count)].reshape(count * rows, cols)


def kernel(sizes, *refs):
    nz, ny, nx, nk = sizes
    (b_hbm, sd_hbm, su_hbm, ld_hbm, lu_hbm, cb_hbm, f_hbm, x_ref, *scratch) = refs
    (
        lm, sm, sut, cb, fac, fsel, sel, kk,
        ev0, ev1, pv, pv1, q0, w0, q1,
        y_dn, y_up, yr_dn, yr_up, t_up, tr, ub, cx, cxr_up, cxr_dn,
        gz, ups, upr, sums, red_c, red_y, red_z,
        load_sem, halo_send, halo_recv, gy_send, gy_recv, gzs_send, gzs_recv,
        u_send, u_recv, rc_send, rc_recv, ry_send, ry_recv, rz_send, rz_recv,
    ) = scratch
    nb = b_hbm.shape[0]
    bs, nr = b_hbm.shape[1:]
    ncb = cb_hbm.shape[0]
    nco = f_hbm.shape[0]
    half = nr // 2
    nrow, ncol = nz * ny, nx * nk
    z, y, x, k = (lax.axis_index(name) for name in ("z", "y", "x", "k"))
    row, col = z * ny + y, x * nk + k
    has_dn, has_up = row > 0, row < nrow - 1

    def row_device(index):
        return {"z": index // ny, "y": lax.rem(index, ny)}

    up_dev = row_device(lax.rem(row + 1, nrow))
    dn_dev = row_device(lax.rem(row + nrow - 1, nrow))

    def col_device(step):
        index = lax.rem(col + step, ncol)
        return {"x": index // nk, "k": lax.rem(index, nk)}

    def y_device(step):
        return {"y": lax.rem(y + step, ny)}

    def z_device(step):
        return {"z": lax.rem(z + step, nz)}

    loads = [
        pltpu.make_async_copy(b_hbm, ev0.at[pl.ds(1, nb)], load_sem.at[0]),
        pltpu.make_async_copy(cb_hbm, cb, load_sem.at[1]),
        pltpu.make_async_copy(lu_hbm, lm.at[pl.ds(0, nb + 1), :, pl.ds(2 * bs, bs)], load_sem.at[2]),
        pltpu.make_async_copy(ld_hbm, lm.at[:, :, pl.ds(bs, bs)], load_sem.at[3]),
        pltpu.make_async_copy(f_hbm, fac, load_sem.at[4]),
        pltpu.make_async_copy(su_hbm, sm.at[:, :, pl.ds(2 * bs, bs)], load_sem.at[5]),
        pltpu.make_async_copy(sd_hbm, sm.at[:, :, pl.ds(bs, bs)], load_sem.at[6]),
    ]
    for load in loads:
        load.start()

    barrier = pltpu.get_barrier_semaphore()
    peers = [up_dev, dn_dev]
    peers += [y_device(s) for s in range(1, ny)]
    peers += [col_device(s) for s in range(1, ncol)]
    peers += [z_device(s) for s in range(1, nz)]
    for peer in peers:
        pl.semaphore_signal(barrier, inc=1, device_id=peer, device_id_type=MESH)

    @pl.when(row == 0)
    def _():
        ev0[0] = jnp.zeros((bs, nr), BF)
        ev1[0] = jnp.zeros((bs, nr), BF)
        yr_dn[...] = jnp.zeros_like(yr_dn)
        tr[...] = jnp.zeros_like(tr)
        cxr_dn[...] = jnp.zeros_like(cxr_dn)

    @pl.when(row == nrow - 1)
    def _():
        ev0[nb + 1] = jnp.zeros((bs, nr), BF)
        ev1[nb + 1] = jnp.zeros((bs, nr), BF)
        pv[nb] = jnp.zeros((bs, nr), BF)
        yr_up[...] = jnp.zeros_like(yr_up)
        cxr_up[...] = jnp.zeros_like(cxr_up)

    rows_of = lax.broadcasted_iota(jnp.int32, sel.shape, 0)
    slots = lax.broadcasted_iota(jnp.int32, sel.shape, 1)
    slot, j = slots // 8, slots % 8
    owner = jnp.where(slot < nrow, slot * ncol + col, row * ncol + (slot - nrow))
    wanted = jnp.where(j < ncb, owner * ncb + j, -1)
    sel[...] = jnp.where(rows_of == wanted, 1.0, 0.0).astype(BF)

    def lanes(h):
        return pl.ds(h * half, half)

    def to_up(index, src, dst):
        return pltpu.make_async_remote_copy(
            src_ref=src, dst_ref=dst, send_sem=halo_send.at[index], recv_sem=halo_recv.at[index],
            device_id=up_dev, device_id_type=MESH,
        )

    def to_dn(index, src, dst):
        return pltpu.make_async_remote_copy(
            src_ref=src, dst_ref=dst, send_sem=halo_send.at[index], recv_sem=halo_recv.at[index],
            device_id=dn_dev, device_id_type=MESH,
        )

    halo = {}
    for h in range(2):
        at = lanes(h)
        edges = [
            (ev0.at[nb, :, at], ev0.at[0, :, at], ev0.at[1, :, at], ev0.at[nb + 1, :, at]),
            (y_up.at[0, :, at], yr_dn.at[0, :, at], y_dn.at[0, :, at], yr_up.at[0, :, at]),
            (t_up.at[:, at], tr.at[:, at], pv.at[0, :, at], pv.at[nb, :, at]),
            (ev1.at[nb, :, at], ev1.at[0, :, at], ev1.at[1, :, at], ev1.at[nb + 1, :, at]),
            (y_up.at[1, :, at], yr_dn.at[1, :, at], y_dn.at[1, :, at], yr_up.at[1, :, at]),
        ]
        for phase, (up_src, up_dst, dn_src, dn_dst) in enumerate(edges):
            index = 4 * phase + 2 * h
            halo[phase, h] = (to_up(index, up_src, up_dst), to_dn(index + 1, dn_src, dn_dst))
    halo[5, 0] = (to_up(20, cx, cxr_dn), to_dn(21, pv1.at[0, :, lanes(0)], cxr_up))

    def send_up(phase, h):
        pl.when(has_up)(lambda: halo[phase, h][0].start())

    def send_dn(phase, h):
        pl.when(has_dn)(lambda: halo[phase, h][1].start())

    def receive(phase, h):
        pl.when(has_dn)(lambda: halo[phase, h][0].wait_recv())
        pl.when(has_up)(lambda: halo[phase, h][1].wait_recv())

    def y_copies(it):
        here = gz.at[it, z, pl.ds(pl.multiple_of(y * 16, 16), 16)]
        return [
            pltpu.make_async_remote_copy(
                src_ref=here, dst_ref=here, send_sem=gy_send.at[it, s], recv_sem=gy_recv.at[it, s],
                device_id=y_device(s), device_id_type=MESH,
            )
            for s in range(1, ny)
        ]

    def z_copies(it):
        here = gz.at[it, z]
        return [
            pltpu.make_async_remote_copy(
                src_ref=here, dst_ref=here, send_sem=gzs_send.at[it, s], recv_sem=gzs_recv.at[it, s],
                device_id=z_device(s), device_id_type=MESH,
            )
            for s in range(1, nz)
        ]

    def u_copies(it):
        copies = []
        for s in range(1, ncol):
            target = lax.rem(col + s, ncol)
            copies.append(
                pltpu.make_async_remote_copy(
                    src_ref=ups.at[it, target], dst_ref=upr.at[it, s],
                    send_sem=u_send.at[it, s], recv_sem=u_recv.at[it, s],
                    device_id=col_device(s), device_id_type=MESH,
                )
            )
        return copies

    gy = [y_copies(it) for it in range(2)]
    gzc = [z_copies(it) for it in range(2)]
    uc = [u_copies(it) for it in range(2)]

    def coarse_rhs(it, vec):
        g = mm(cb[...], stacked(vec, 1, nb))
        g = jnp.concatenate([g, jnp.zeros((8 - ncb, nr), F32)], axis=0)
        packed = jnp.concatenate([g[:, :half], g[:, half:]], axis=0).astype(BF)
        gz[it, z, pl.ds(pl.multiple_of(y * 16, 16), 16)] = packed

    def coarse_begin(it):
        for copy in gy[it]:
            copy.start()

    def coarse_spread_rows(it):
        for copy in gy[it]:
            copy.wait_recv()
        for copy in gzc[it]:
            copy.start()

    def coarse_solve(it):
        for copy in gzc[it]:
            copy.wait_recv()
        got = gz[it].astype(F32).reshape(nrow, 16, half)
        sides = [got[:, 8 * h : 8 * h + 8].reshape(nrow * 8, half) for h in range(2)]
        g = jnp.concatenate(sides, axis=1).astype(BF)
        u = mm(kk[0], g) + mm(kk[1], g)
        ups[it] = u.reshape(ncol, 8, nr)
        for copy in uc[it]:
            copy.start()

    def coarse_end(it):
        for copy in uc[it]:
            copy.wait_recv()
        u = ups[it, pl.ds(col, 1)].reshape(8, nr)
        for s in range(1, ncol):
            u = u + upr[it, s]
        return u[:ncb].astype(BF)

    def spread(layer, u):
        return lax.dot_general(
            cb[:, pl.ds(pl.multiple_of(layer * bs, bs), bs)], u, (((0,), (0,)), ((), ())),
            preferred_element_type=F32,
        )

    loads[0].wait()
    loads[1].wait()
    coarse_rhs(0, ev0)
    pl.semaphore_wait(barrier, len(peers))
    coarse_begin(0)
    for h in range(2):
        send_up(0, h)
        send_dn(0, h)

    loads[2].wait()

    @pl.loop(0, nb + 1)
    def _(i):
        lm[i + 1, :, pl.ds(0, bs)] = lm[i, :, pl.ds(2 * bs, bs)].T

    coarse_spread_rows(0)

    loads[3].wait()

    def half_of(ref, start, count, h):
        return ref[pl.ds(start, count), :, lanes(h)].reshape(count * bs, half)

    def local_middle(vec, out):
        @pl.loop(2, nb)
        def _(i):
            out[i - 1] = mm(lm[i], stacked(vec, i - 1, 3))

    def local_margins(it, vec):
        for h in range(2):
            receive(3 * it, h)
            y_dn[it, :, lanes(h)] = mm(lm[0, :, pl.ds(bs, 2 * bs)], half_of(vec, 0, 2, h)).astype(BF)
            send_dn(3 * it + 1, h)
            y_up[it, :, lanes(h)] = mm(lm[nb + 1, :, pl.ds(0, 2 * bs)], half_of(vec, nb, 2, h)).astype(BF)
            send_up(3 * it + 1, h)

    def local_edges(vec, out):
        @pl.loop(0, 2)
        def _(e):
            i = 1 + e * (nb - 1)
            out[i - 1] = mm(lm[i], stacked(vec, i - 1, 3))

    local_middle(ev0, q0)
    local_margins(0, ev0)

    loads[4].wait()

    @pl.loop(0, nco // 256)
    def _(i):
        at = pl.ds(pl.multiple_of(i * 256, 256), 256)
        fsel[at, :] = mm(fac[at, :], sel[...]).astype(BF)

    split = nrow * 8
    kmat = lax.dot_general(
        fsel[:, split:], fsel[:, :split], (((0,), (0,)), ((), ())), preferred_element_type=F32
    )
    kk[0] = kmat.astype(BF)
    kk[1] = (kmat - kmat.astype(BF).astype(F32)).astype(BF)
    coarse_solve(0)
    local_edges(ev0, q0)

    loads[5].wait()

    @pl.loop(0, nb)
    def _(i):
        sut[i] = sm[i, :, pl.ds(2 * bs, bs)].T

    @pl.loop(1, nb)
    def _(i):
        sm[i, :, pl.ds(0, bs)] = sut[i - 1]

    loads[6].wait()

    def finish(it, out, u, vec, send):
        for h in range(2):
            receive(3 * it + 1, h)
            for layer, came in ((0, yr_dn), (nb - 1, yr_up)):
                total = out[layer, :, lanes(h)] + came[it, :, lanes(h)].astype(F32)
                total = total + spread(layer, u[:, h * half : (h + 1) * half])
                out[layer, :, lanes(h)] = total
                vec[layer, :, lanes(h)] = total.astype(BF)
            send(h)

        @pl.loop(1, nb - 1)
        def _(i):
            total = out[i] + spread(i, u)
            out[i] = total
            vec[i] = total.astype(BF)

    def send_direction(h):
        send_dn(2, h)
        t_up[:, lanes(h)] = mm(sut[nb - 1], pv[nb - 1, :, lanes(h)]).astype(BF)
        send_up(2, h)

    finish(0, q0, coarse_end(0), pv, send_direction)

    def stiff_inside(vec, store):
        store(0, mm(sm[0, :, pl.ds(bs, 2 * bs)], stacked(vec, 0, 2)))
        for i in range(1, nb - 1):
            store(i, mm(sm[i], stacked(vec, i - 1, 3)))
        store(nb - 1, mm(sm[nb - 1, :, pl.ds(0, 2 * bs)], stacked(vec, nb - 2, 2)))

    def store_w0(i, value):
        w0[i] = value

    stiff_inside(pv, store_w0)
    for i in range(1, nb - 1):
        ev1[1 + i] = w0[i].astype(BF)
    for h in range(2):
        at = lanes(h)
        receive(2, h)
        ub[:, at] = mm(sm[nb - 1, :, pl.ds(2 * bs, bs)], pv[nb, :, at])
        low = w0[0, :, at] + tr[:, at].astype(F32)
        high = w0[nb - 1, :, at] + ub[:, at]
        w0[0, :, at] = low
        w0[nb - 1, :, at] = high
        ev1[1, :, at] = low.astype(BF)
        ev1[nb, :, at] = high.astype(BF)
        if h == 1:
            coarse_rhs(1, ev1)
            coarse_begin(1)
        send_dn(3, h)
        send_up(3, h)

    def columns(value):
        return jnp.sum(value, axis=0, keepdims=True)

    s1 = jnp.zeros((1, nr), F32)
    s2 = jnp.zeros((1, nr), F32)
    for i in range(nb):
        s1 = s1 + columns(ev0[1 + i].astype(F32) * q0[i])
        s2 = s2 + columns(w0[i] * q0[i])

    local_middle(ev1, q1)
    coarse_spread_rows(1)
    local_margins(1, ev1)
    local_edges(ev1, q1)
    coarse_solve(1)

    def send_cross(h):
        if h == 0:
            send_dn(5, 0)
        else:
            cx[...] = mm(sut[nb - 1], pv1[nb - 1, :, lanes(1)]).astype(BF)
            send_up(5, 0)

    finish(1, q1, coarse_end(1), pv1, send_cross)

    s3 = jnp.zeros((1, nr), F32)
    s4 = jnp.zeros((1, nr), F32)
    for i in range(nb):
        s3 = s3 + columns(ev0[1 + i].astype(F32) * q1[i])
        s4 = s4 + columns(w0[i] * q1[i])
    s5 = columns(tr[...].astype(F32) * q1[0]) + columns(ub[...] * q1[nb - 1])
    mixed = []

    def add_dots(i, value):
        mixed.append((columns(q0[i] * value), columns(q1[i] * value)))

    stiff_inside(pv1, add_dots)
    s5 = s5 + sum(pair[0] for pair in mixed)
    s6 = sum(pair[1] for pair in mixed)
    receive(5, 0)
    from_up = mm(sm[nb - 1, :, pl.ds(2 * bs, bs)], cxr_up[...])
    cross_up = columns(from_up * q1[nb - 1, :, pl.ds(0, half)])
    cross_dn = columns(cxr_dn[...].astype(F32) * q1[0, :, pl.ds(half, half)])
    s6 = s6 + 2.0 * jnp.concatenate([cross_up, cross_dn], axis=1)

    sums[0] = jnp.concatenate([s1, s2, s3, s4, s5, s6, jnp.zeros((2, nr), F32)], axis=0)

    def reduce_stage(stage, buf, device, count, send, recv):
        copies = [
            pltpu.make_async_remote_copy(
                src_ref=sums.at[stage], dst_ref=buf.at[s], send_sem=send.at[s], recv_sem=recv.at[s],
                device_id=device(s), device_id_type=MESH,
            )
            for s in range(1, count)
        ]
        for copy in copies:
            copy.start()
        total = sums[stage]
        for s, copy in enumerate(copies, 1):
            copy.wait_recv()
            total = total + buf[s]
        return copies, total

    sent_c, total = reduce_stage(0, red_c, col_device, ncol, rc_send, rc_recv)
    sums[1] = total
    sent_y, total = reduce_stage(1, red_y, y_device, ny, ry_send, ry_recv)
    sums[2] = total
    sent_z, total = reduce_stage(2, red_z, z_device, nz, rz_send, rz_recv)

    d = [total[i : i + 1] for i in range(6)]
    alpha = d[0] / d[1]
    rho = d[0] - alpha * (d[2] + d[1]) + alpha * alpha * d[3]
    grow = 1.0 + rho / d[0]
    denom = grow * grow * d[1] - grow * alpha * (d[4] + d[3]) + alpha * alpha * d[5]
    step = rho / denom
    c0 = jnp.broadcast_to(alpha + step * grow, (bs, nr))
    c1 = jnp.broadcast_to(alpha * step, (bs, nr))
    for i in range(nb):
        x_ref[i] = c0 * q0[i] - c1 * q1[i]

    for copy in sent_c + sent_y + sent_z + gy[0] + gy[1] + gzc[0] + gzc[1] + uc[0] + uc[1]:
        copy.wait_send()
    for up, dn in halo.values():
        pl.when(has_up)(lambda up=up: up.wait_send())
        pl.when(has_dn)(lambda dn=dn: dn.wait_send())


def on_device(sizes, b, sd, su, ld, lu, cb, fac):
    nz, ny, nx, nk = sizes
    b, sd, su, ld, lu = (a[:, 0] for a in (b, sd, su, ld, lu))
    cb = cb[0, 0]
    nb, bs, nr = b.shape
    ncb = cb.shape[0]
    nco = fac.shape[0]
    nrow, ncol = nz * ny, nx * nk
    half = nr // 2
    nsel = 8 * (nrow + ncol)
    dma = pltpu.SemaphoreType.DMA
    vm = pltpu.VMEM
    scratch = [
        vm((nb + 2, bs, 3 * bs), BF),
        vm((nb, bs, 3 * bs), BF),
        vm((nb, bs, bs), BF),
        vm((ncb, nb * bs), BF),
        vm((nco, nco), BF),
        vm((nco, nsel), BF),
        vm((nco, nsel), BF),
        vm((2, 8 * ncol, 8 * nrow), BF),
        vm((nb + 2, bs, nr), BF),
        vm((nb + 2, bs, nr), BF),
        vm((nb + 1, bs, nr), BF),
        vm((nb, bs, nr), BF),
        vm((nb, bs, nr), F32),
        vm((nb, bs, nr), F32),
        vm((nb, bs, nr), F32),
        vm((2, bs, nr), BF),
        vm((2, bs, nr), BF),
        vm((2, bs, nr), BF),
        vm((2, bs, nr), BF),
        vm((bs, nr), BF),
        vm((bs, nr), BF),
        vm((bs, nr), F32),
        vm((bs, half), BF),
        vm((bs, half), BF),
        vm((bs, half), BF),
        vm((2, nz, ny * 16, half), BF),
        vm((2, ncol, 8, nr), F32),
        vm((2, ncol, 8, nr), F32),
        vm((3, 8, nr), F32),
        vm((ncol, 8, nr), F32),
        vm((ny, 8, nr), F32),
        vm((nz, 8, nr), F32),
        dma((7,)),
        dma((22,)),
        dma((22,)),
        dma((2, ny)),
        dma((2, ny)),
        dma((2, nz)),
        dma((2, nz)),
        dma((2, ncol)),
        dma((2, ncol)),
        dma((ncol,)),
        dma((ncol,)),
        dma((ny,)),
        dma((ny,)),
        dma((nz,)),
        dma((nz,)),
    ]
    out = pl.pallas_call(
        functools.partial(kernel, sizes),
        out_shape=jax.ShapeDtypeStruct((nb, bs, nr), F32),
        in_specs=[pl.BlockSpec(memory_space=pl.ANY)] * 7,
        out_specs=pl.BlockSpec(memory_space=pltpu.VMEM),
        scratch_shapes=scratch,
        compiler_params=pltpu.CompilerParams(
            collective_id=0, has_side_effects=True, vmem_limit_bytes=60 * 1024 * 1024
        ),
        name="schwarz_pcg",
    )(b, sd, su, ld, lu, cb, fac)
    return out[:, None]


def solution(mesh):
    sizes = (8, 4, 4, 2)
    if mesh.devices.size != 256:
        sizes = (2, 2, 2, 2)
    split = Mesh(mesh.devices.reshape(sizes), ("z", "y", "x", "k"))
    row, col = ("z", "y"), ("x", "k")
    spec = P(row, col, None, None)
    return jax.shard_map(
        functools.partial(on_device, sizes),
        mesh=split,
        in_specs=(spec,) * 6 + (P(),),
        out_specs=spec,
        check_vma=False,
    )
```

```python
import functools

import jax
import jax.numpy as jnp
from jax import lax
from jax.experimental import pallas as pl
from jax.experimental.pallas import tpu as pltpu
from jax.sharding import Mesh
from jax.sharding import PartitionSpec as P

MESH = pl.DeviceIdType.MESH
F32 = jnp.float32
BF = jnp.bfloat16


def mm(left, right):
    return jnp.dot(left, right, preferred_element_type=F32)


def stacked(ref, start, count):
    _, rows, cols = ref.shape
    return ref[pl.ds(start, count)].reshape(count * rows, cols)


def kernel(sizes, *refs):
    nz, ny, nx, nk = sizes
    (b_hbm, sd_hbm, su_hbm, ld_hbm, lu_hbm, cb_hbm, f_hbm, x_ref, *scratch) = refs
    (
        lm, sm, sut, cb, fac, fsel, sel, kk,
        ev0, ev1, pv, pv1, q0, w0, q1,
        y_dn, y_up, yr_dn, yr_up, t_up, tr, trf, ub, cx, cxr_up, cxr_dn,
        ed, ed1, stat, statr, wup, us, usr,
        gz, ups, upr, sums, red_c, red_y, red_z,
        load_sem, halo_send, halo_recv, gy_send, gy_recv, gzs_send, gzs_recv,
        u_send, u_recv, rc_send, rc_recv, ry_send, ry_recv, rz_send, rz_recv,
    ) = scratch
    nb = b_hbm.shape[0]
    bs, nr = b_hbm.shape[1:]
    ncb = cb_hbm.shape[0]
    nco = f_hbm.shape[0]
    half = nr // 2
    nrow, ncol = nz * ny, nx * nk
    z, y, x, k = (lax.axis_index(name) for name in ("z", "y", "x", "k"))
    row, col = z * ny + y, x * nk + k
    has_dn, has_up = row > 0, row < nrow - 1

    def row_device(index):
        return {"z": index // ny, "y": lax.rem(index, ny)}

    up_dev = row_device(lax.rem(row + 1, nrow))
    dn_dev = row_device(lax.rem(row + nrow - 1, nrow))

    def col_device(step):
        index = lax.rem(col + step, ncol)
        return {"x": index // nk, "k": lax.rem(index, nk)}

    def y_device(step):
        return {"y": lax.rem(y + step, ny)}

    def z_device(step):
        return {"z": lax.rem(z + step, nz)}

    loads = [
        pltpu.make_async_copy(b_hbm, ev0.at[pl.ds(1, nb)], load_sem.at[0]),
        pltpu.make_async_copy(cb_hbm, cb, load_sem.at[1]),
        pltpu.make_async_copy(lu_hbm, lm.at[pl.ds(0, nb + 1), :, pl.ds(2 * bs, bs)], load_sem.at[2]),
        pltpu.make_async_copy(ld_hbm, lm.at[:, :, pl.ds(bs, bs)], load_sem.at[3]),
        pltpu.make_async_copy(f_hbm, fac, load_sem.at[4]),
        pltpu.make_async_copy(su_hbm, sm.at[:, :, pl.ds(2 * bs, bs)], load_sem.at[5]),
        pltpu.make_async_copy(sd_hbm, sm.at[:, :, pl.ds(bs, bs)], load_sem.at[6]),
    ]
    for load in loads:
        load.start()

    barrier = pltpu.get_barrier_semaphore()
    peers = [up_dev, dn_dev]
    peers += [y_device(s) for s in range(1, ny)]
    peers += [col_device(s) for s in range(1, ncol)]
    peers += [z_device(s) for s in range(1, nz)]
    for peer in peers:
        pl.semaphore_signal(barrier, inc=1, device_id=peer, device_id_type=MESH)

    @pl.when(row == 0)
    def _():
        ev0[0] = jnp.zeros((bs, nr), BF)
        ev1[0] = jnp.zeros((bs, nr), BF)
        yr_dn[...] = jnp.zeros_like(yr_dn)
        tr[...] = jnp.zeros_like(tr)
        cxr_dn[...] = jnp.zeros_like(cxr_dn)
        statr[0] = jnp.zeros(statr.shape[1:], BF)
        usr[0] = jnp.zeros(usr.shape[1:], BF)

    @pl.when(row == nrow - 1)
    def _():
        ev0[nb + 1] = jnp.zeros((bs, nr), BF)
        ev1[nb + 1] = jnp.zeros((bs, nr), BF)
        pv[nb] = jnp.zeros((bs, nr), BF)
        yr_up[...] = jnp.zeros_like(yr_up)
        cxr_up[...] = jnp.zeros_like(cxr_up)
        statr[1] = jnp.zeros(statr.shape[1:], BF)
        usr[1] = jnp.zeros(usr.shape[1:], BF)

    rows_of = lax.broadcasted_iota(jnp.int32, sel.shape, 0)
    slots = lax.broadcasted_iota(jnp.int32, sel.shape, 1)
    slot, j = slots // 8, slots % 8
    owner = jnp.where(slot < nrow, slot * ncol + col, row * ncol + (slot - nrow))
    wanted = jnp.where(j < ncb, owner * ncb + j, -1)
    sel[...] = jnp.where(rows_of == wanted, 1.0, 0.0).astype(BF)

    def lanes(h):
        return pl.ds(h * half, half)

    def to_up(index, src, dst):
        return pltpu.make_async_remote_copy(
            src_ref=src, dst_ref=dst, send_sem=halo_send.at[index], recv_sem=halo_recv.at[index],
            device_id=up_dev, device_id_type=MESH,
        )

    def to_dn(index, src, dst):
        return pltpu.make_async_remote_copy(
            src_ref=src, dst_ref=dst, send_sem=halo_send.at[index], recv_sem=halo_recv.at[index],
            device_id=dn_dev, device_id_type=MESH,
        )

    halo = {}
    for h in range(2):
        at = lanes(h)
        edges = [
            (ev0.at[nb, :, at], ev0.at[0, :, at], ev0.at[1, :, at], ev0.at[nb + 1, :, at]),
            (y_up.at[0, :, at], yr_dn.at[0, :, at], y_dn.at[0, :, at], yr_up.at[0, :, at]),
            (t_up.at[:, at], tr.at[:, at], ed.at[:, at], pv.at[nb, :, at]),
            (ev1.at[nb, :, at], ev1.at[0, :, at], ev1.at[1, :, at], ev1.at[nb + 1, :, at]),
            (y_up.at[1, :, at], yr_dn.at[1, :, at], y_dn.at[1, :, at], yr_up.at[1, :, at]),
        ]
        for phase, (up_src, up_dst, dn_src, dn_dst) in enumerate(edges):
            index = 4 * phase + 2 * h
            halo[phase, h] = (to_up(index, up_src, up_dst), to_dn(index + 1, dn_src, dn_dst))
    halo[5, 0] = (to_up(20, cx, cxr_dn), to_dn(21, ed1, cxr_up))
    halo[6, 0] = (to_up(22, stat.at[0], statr.at[0]), to_dn(23, stat.at[1], statr.at[1]))
    for it in range(2):
        index = 24 + 2 * it
        halo[7 + it, 0] = (
            to_up(index, us.at[it], usr.at[0, it]),
            to_dn(index + 1, us.at[it], usr.at[1, it]),
        )

    def send_up(phase, h):
        pl.when(has_up)(lambda: halo[phase, h][0].start())

    def send_dn(phase, h):
        pl.when(has_dn)(lambda: halo[phase, h][1].start())

    def receive(phase, h):
        pl.when(has_dn)(lambda: halo[phase, h][0].wait_recv())
        pl.when(has_up)(lambda: halo[phase, h][1].wait_recv())

    def y_copies(it):
        here = gz.at[it, z, pl.ds(pl.multiple_of(y * 16, 16), 16)]
        return [
            pltpu.make_async_remote_copy(
                src_ref=here, dst_ref=here, send_sem=gy_send.at[it, s], recv_sem=gy_recv.at[it, s],
                device_id=y_device(s), device_id_type=MESH,
            )
            for s in range(1, ny)
        ]

    def z_copies(it):
        here = gz.at[it, z]
        return [
            pltpu.make_async_remote_copy(
                src_ref=here, dst_ref=here, send_sem=gzs_send.at[it, s], recv_sem=gzs_recv.at[it, s],
                device_id=z_device(s), device_id_type=MESH,
            )
            for s in range(1, nz)
        ]

    def u_copies(it):
        copies = []
        for s in range(1, ncol):
            target = lax.rem(col + s, ncol)
            copies.append(
                pltpu.make_async_remote_copy(
                    src_ref=ups.at[it, target], dst_ref=upr.at[it, s],
                    send_sem=u_send.at[it, s], recv_sem=u_recv.at[it, s],
                    device_id=col_device(s), device_id_type=MESH,
                )
            )
        return copies

    gy = [y_copies(it) for it in range(2)]
    gzc = [z_copies(it) for it in range(2)]
    uc = [u_copies(it) for it in range(2)]

    def coarse_rhs(it, vec):
        g = mm(cb[...], stacked(vec, 1, nb))
        g = jnp.concatenate([g, jnp.zeros((8 - ncb, nr), F32)], axis=0)
        packed = jnp.concatenate([g[:, :half], g[:, half:]], axis=0).astype(BF)
        gz[it, z, pl.ds(pl.multiple_of(y * 16, 16), 16)] = packed

    def coarse_begin(it):
        for copy in gy[it]:
            copy.start()

    def coarse_spread_rows(it):
        for copy in gy[it]:
            copy.wait_recv()
        for copy in gzc[it]:
            copy.start()

    def coarse_solve(it):
        for copy in gzc[it]:
            copy.wait_recv()
        got = gz[it].astype(F32).reshape(nrow, 16, half)
        sides = [got[:, 8 * h : 8 * h + 8].reshape(nrow * 8, half) for h in range(2)]
        g = jnp.concatenate(sides, axis=1).astype(BF)
        u = mm(kk[0], g) + mm(kk[1], g)
        ups[it] = u.reshape(ncol, 8, nr)
        for copy in uc[it]:
            copy.start()

    def coarse_end(it):
        for copy in uc[it]:
            copy.wait_recv()
        u = ups[it, pl.ds(col, 1)].reshape(8, nr)
        for s in range(1, ncol):
            u = u + upr[it, s]
        return u

    def spread(layer, u):
        return lax.dot_general(
            cb[:, pl.ds(pl.multiple_of(layer * bs, bs), bs)], u, (((0,), (0,)), ((), ())),
            preferred_element_type=F32,
        )

    loads[0].wait()
    loads[1].wait()
    coarse_rhs(0, ev0)
    pl.semaphore_wait(barrier, len(peers))
    coarse_begin(0)
    for h in range(2):
        send_up(0, h)
        send_dn(0, h)

    loads[2].wait()

    @pl.loop(0, nb + 1)
    def _(i):
        lm[i + 1, :, pl.ds(0, bs)] = lm[i, :, pl.ds(2 * bs, bs)].T

    coarse_spread_rows(0)

    loads[3].wait()

    def half_of(ref, start, count, h):
        return ref[pl.ds(start, count), :, lanes(h)].reshape(count * bs, half)

    def local_middle(vec, out):
        @pl.loop(2, nb)
        def _(i):
            out[i - 1] = mm(lm[i], stacked(vec, i - 1, 3))

    def local_margins(it, vec):
        for h in range(2):
            receive(3 * it, h)
            y_dn[it, :, lanes(h)] = mm(lm[0, :, pl.ds(bs, 2 * bs)], half_of(vec, 0, 2, h)).astype(BF)
            send_dn(3 * it + 1, h)
            y_up[it, :, lanes(h)] = mm(lm[nb + 1, :, pl.ds(0, 2 * bs)], half_of(vec, nb, 2, h)).astype(BF)
            send_up(3 * it + 1, h)

    def local_edges(vec, out):
        @pl.loop(0, 2)
        def _(e):
            i = 1 + e * (nb - 1)
            out[i - 1] = mm(lm[i], stacked(vec, i - 1, 3))

    local_middle(ev0, q0)
    local_margins(0, ev0)

    loads[4].wait()

    @pl.loop(0, nco // 256)
    def _(i):
        at = pl.ds(pl.multiple_of(i * 256, 256), 256)
        fsel[at, :] = mm(fac[at, :], sel[...]).astype(BF)

    split = nrow * 8
    kmat = lax.dot_general(
        fsel[:, split:], fsel[:, :split], (((0,), (0,)), ((), ())), preferred_element_type=F32
    )
    kk[0] = kmat.astype(BF)
    kk[1] = (kmat - kmat.astype(BF).astype(F32)).astype(BF)
    coarse_solve(0)
    local_edges(ev0, q0)

    loads[5].wait()

    @pl.loop(0, nb)
    def _(i):
        sut[i] = sm[i, :, pl.ds(2 * bs, bs)].T

    @pl.loop(1, nb)
    def _(i):
        sm[i, :, pl.ds(0, bs)] = sut[i - 1]

    def two_pieces(value):
        top = value.astype(BF).astype(F32)
        return jnp.concatenate([top, value - top], axis=0).astype(BF)

    pad = jnp.zeros((8 - ncb, bs), F32)
    upper = sm[nb - 1, :, pl.ds(2 * bs, bs)]
    stat[0] = two_pieces(jnp.concatenate([mm(cb[:, pl.ds((nb - 1) * bs, bs)], upper), pad], axis=0))
    lowest = cb[:, pl.ds(0, bs)].astype(F32)
    stat[1] = jnp.concatenate([lowest, pad, jnp.zeros((8, bs), F32)], axis=0).astype(BF)
    send_up(6, 0)
    send_dn(6, 0)

    def finish_local(it, out, send):
        for h in range(2):
            at = lanes(h)
            receive(3 * it + 1, h)
            out[0, :, at] += yr_dn[it, :, at].astype(F32)
            out[nb - 1, :, at] += yr_up[it, :, at].astype(F32)
            send(h)

    def finish_coarse(it, out, vec):
        u = coarse_end(it)
        us[it] = jnp.concatenate([u, u], axis=0).astype(BF)
        send_up(7 + it, 0)
        send_dn(7 + it, 0)
        mine = u[:ncb].astype(BF)

        @pl.loop(0, nb)
        def _(i):
            total = out[i] + spread(i, mine)
            out[i] = total
            vec[i] = total.astype(BF)

    def couple(left, u):
        return lax.dot_general(left, u, (((0,), (0,)), ((), ())), preferred_element_type=F32)

    def send_direction(h):
        at = lanes(h)
        ed[:, at] = q0[0, :, at].astype(BF)
        send_dn(2, h)
        t_up[:, at] = mm(sut[nb - 1], q0[nb - 1, :, at].astype(BF)).astype(BF)
        send_up(2, h)

    finish_local(0, q0, send_direction)
    loads[6].wait()
    receive(6, 0)
    wup[...] = two_pieces(mm(statr[1], sut[nb - 1])[:8])
    finish_coarse(0, q0, pv)

    def stiff_inside(vec, store):
        store(0, mm(sm[0, :, pl.ds(bs, 2 * bs)], stacked(vec, 0, 2)))
        for i in range(1, nb - 1):
            store(i, mm(sm[i], stacked(vec, i - 1, 3)))
        store(nb - 1, mm(sm[nb - 1, :, pl.ds(0, 2 * bs)], stacked(vec, nb - 2, 2)))

    def store_w0(i, value):
        w0[i] = value

    stiff_inside(pv, store_w0)
    for i in range(1, nb - 1):
        ev1[1 + i] = w0[i].astype(BF)
    for h in range(2):
        at = lanes(h)
        receive(2, h)
        ub[:, at] = mm(sm[nb - 1, :, pl.ds(2 * bs, bs)], pv[nb, :, at])
        if h == 0:
            receive(7, 0)
        ub[:, at] += couple(wup[...], usr[1, 0, :, at])
        trf[:, at] = tr[:, at].astype(F32) + couple(statr[0], usr[0, 0, :, at])
        low = w0[0, :, at] + trf[:, at]
        high = w0[nb - 1, :, at] + ub[:, at]
        w0[0, :, at] = low
        w0[nb - 1, :, at] = high
        ev1[1, :, at] = low.astype(BF)
        ev1[nb, :, at] = high.astype(BF)
        if h == 1:
            coarse_rhs(1, ev1)
            coarse_begin(1)
        send_dn(3, h)
        send_up(3, h)

    def columns(value):
        return jnp.sum(value, axis=0, keepdims=True)

    s1 = jnp.zeros((1, nr), F32)
    s2 = jnp.zeros((1, nr), F32)
    for i in range(nb):
        s1 = s1 + columns(ev0[1 + i].astype(F32) * q0[i])
        s2 = s2 + columns(w0[i] * q0[i])

    local_middle(ev1, q1)
    coarse_spread_rows(1)
    local_margins(1, ev1)
    local_edges(ev1, q1)
    coarse_solve(1)

    def send_cross(h):
        if h == 0:
            ed1[...] = q1[0, :, lanes(0)].astype(BF)
            send_dn(5, 0)
        else:
            cx[...] = mm(sut[nb - 1], q1[nb - 1, :, lanes(1)].astype(BF)).astype(BF)
            send_up(5, 0)

    finish_local(1, q1, send_cross)
    finish_coarse(1, q1, pv1)

    s3 = jnp.zeros((1, nr), F32)
    s4 = jnp.zeros((1, nr), F32)
    for i in range(nb):
        s3 = s3 + columns(ev0[1 + i].astype(F32) * q1[i])
        s4 = s4 + columns(w0[i] * q1[i])
    s5 = columns(trf[...] * q1[0]) + columns(ub[...] * q1[nb - 1])
    mixed = []

    def add_dots(i, value):
        mixed.append((columns(q0[i] * value), columns(q1[i] * value)))

    stiff_inside(pv1, add_dots)
    s5 = s5 + sum(pair[0] for pair in mixed)
    s6 = sum(pair[1] for pair in mixed)
    receive(5, 0)
    from_up = mm(sm[nb - 1, :, pl.ds(2 * bs, bs)], cxr_up[...])
    receive(8, 0)
    from_up = from_up + couple(wup[...], usr[1, 1, :, lanes(0)])
    from_dn = cxr_dn[...].astype(F32) + couple(statr[0], usr[0, 1, :, lanes(1)])
    cross_up = columns(from_up * q1[nb - 1, :, pl.ds(0, half)])
    cross_dn = columns(from_dn * q1[0, :, pl.ds(half, half)])
    s6 = s6 + 2.0 * jnp.concatenate([cross_up, cross_dn], axis=1)

    sums[0] = jnp.concatenate([s1, s2, s3, s4, s5, s6, jnp.zeros((2, nr), F32)], axis=0)

    def reduce_stage(stage, buf, device, count, send, recv):
        copies = [
            pltpu.make_async_remote_copy(
                src_ref=sums.at[stage], dst_ref=buf.at[s], send_sem=send.at[s], recv_sem=recv.at[s],
                device_id=device(s), device_id_type=MESH,
            )
            for s in range(1, count)
        ]
        for copy in copies:
            copy.start()
        total = sums[stage]
        for s, copy in enumerate(copies, 1):
            copy.wait_recv()
            total = total + buf[s]
        return copies, total

    sent_c, total = reduce_stage(0, red_c, col_device, ncol, rc_send, rc_recv)
    sums[1] = total
    sent_y, total = reduce_stage(1, red_y, y_device, ny, ry_send, ry_recv)
    sums[2] = total
    sent_z, total = reduce_stage(2, red_z, z_device, nz, rz_send, rz_recv)

    d = [total[i : i + 1] for i in range(6)]
    alpha = d[0] / d[1]
    rho = d[0] - alpha * (d[2] + d[1]) + alpha * alpha * d[3]
    grow = 1.0 + rho / d[0]
    denom = grow * grow * d[1] - grow * alpha * (d[4] + d[3]) + alpha * alpha * d[5]
    step = rho / denom
    c0 = jnp.broadcast_to(alpha + step * grow, (bs, nr))
    c1 = jnp.broadcast_to(alpha * step, (bs, nr))
    for i in range(nb):
        x_ref[i] = c0 * q0[i] - c1 * q1[i]

    for copy in sent_c + sent_y + sent_z + gy[0] + gy[1] + gzc[0] + gzc[1] + uc[0] + uc[1]:
        copy.wait_send()
    for up, dn in halo.values():
        pl.when(has_up)(lambda up=up: up.wait_send())
        pl.when(has_dn)(lambda dn=dn: dn.wait_send())


def on_device(sizes, b, sd, su, ld, lu, cb, fac):
    nz, ny, nx, nk = sizes
    b, sd, su, ld, lu = (a[:, 0] for a in (b, sd, su, ld, lu))
    cb = cb[0, 0]
    nb, bs, nr = b.shape
    ncb = cb.shape[0]
    nco = fac.shape[0]
    nrow, ncol = nz * ny, nx * nk
    half = nr // 2
    nsel = 8 * (nrow + ncol)
    dma = pltpu.SemaphoreType.DMA
    vm = pltpu.VMEM
    scratch = [
        vm((nb + 2, bs, 3 * bs), BF),
        vm((nb, bs, 3 * bs), BF),
        vm((nb, bs, bs), BF),
        vm((ncb, nb * bs), BF),
        vm((nco, nco), BF),
        vm((nco, nsel), BF),
        vm((nco, nsel), BF),
        vm((2, 8 * ncol, 8 * nrow), BF),
        vm((nb + 2, bs, nr), BF),
        vm((nb + 2, bs, nr), BF),
        vm((nb + 1, bs, nr), BF),
        vm((nb, bs, nr), BF),
        vm((nb, bs, nr), F32),
        vm((nb, bs, nr), F32),
        vm((nb, bs, nr), F32),
        vm((2, bs, nr), BF),
        vm((2, bs, nr), BF),
        vm((2, bs, nr), BF),
        vm((2, bs, nr), BF),
        vm((bs, nr), BF),
        vm((bs, nr), BF),
        vm((bs, nr), F32),
        vm((bs, nr), F32),
        vm((bs, half), BF),
        vm((bs, half), BF),
        vm((bs, half), BF),
        vm((bs, nr), BF),
        vm((bs, half), BF),
        vm((2, 16, bs), BF),
        vm((2, 16, bs), BF),
        vm((16, bs), BF),
        vm((2, 16, nr), BF),
        vm((2, 2, 16, nr), BF),
        vm((2, nz, ny * 16, half), BF),
        vm((2, ncol, 8, nr), F32),
        vm((2, ncol, 8, nr), F32),
        vm((3, 8, nr), F32),
        vm((ncol, 8, nr), F32),
        vm((ny, 8, nr), F32),
        vm((nz, 8, nr), F32),
        dma((7,)),
        dma((28,)),
        dma((28,)),
        dma((2, ny)),
        dma((2, ny)),
        dma((2, nz)),
        dma((2, nz)),
        dma((2, ncol)),
        dma((2, ncol)),
        dma((ncol,)),
        dma((ncol,)),
        dma((ny,)),
        dma((ny,)),
        dma((nz,)),
        dma((nz,)),
    ]
    out = pl.pallas_call(
        functools.partial(kernel, sizes),
        out_shape=jax.ShapeDtypeStruct((nb, bs, nr), F32),
        in_specs=[pl.BlockSpec(memory_space=pl.ANY)] * 7,
        out_specs=pl.BlockSpec(memory_space=pltpu.VMEM),
        scratch_shapes=scratch,
        compiler_params=pltpu.CompilerParams(
            collective_id=0, has_side_effects=True, vmem_limit_bytes=60 * 1024 * 1024
        ),
        name="schwarz_pcg",
    )(b, sd, su, ld, lu, cb, fac)
    return out[:, None]


def solution(mesh):
    sizes = (8, 4, 4, 2)
    if mesh.devices.size != 256:
        sizes = (2, 2, 2, 2)
    split = Mesh(mesh.devices.reshape(sizes), ("z", "y", "x", "k"))
    row, col = ("z", "y"), ("x", "k")
    spec = P(row, col, None, None)
    return jax.shard_map(
        functools.partial(on_device, sizes),
        mesh=split,
        in_specs=(spec,) * 6 + (P(),),
        out_specs=spec,
        check_vma=False,
    )
```

```python
import functools

import jax
import jax.numpy as jnp
from jax import lax
from jax.experimental import pallas as pl
from jax.experimental.pallas import tpu as pltpu
from jax.sharding import Mesh
from jax.sharding import PartitionSpec as P

MESH = pl.DeviceIdType.MESH
F32 = jnp.float32
BF = jnp.bfloat16


def mm(left, right):
    return jnp.dot(left, right, preferred_element_type=F32)


def stacked(ref, start, count):
    _, rows, cols = ref.shape
    return ref[pl.ds(start, count)].reshape(count * rows, cols)


def kernel(sizes, *refs):
    nz, ny, nx, nk = sizes
    (b_hbm, sd_hbm, su_hbm, ld_hbm, lu_hbm, cb_hbm, f_hbm, x_ref, *scratch) = refs
    (
        lm, sm, sut, cb, fac, fsel, sel, kk,
        ev0, ev1, pv, pv1, q0, w0, q1,
        y_dn, y_up, yr_dn, yr_up, t_up, tr, trf, ub, cx, cxr_up, cxr_dn,
        ed, ed1, stat, statr, wup, us, usr,
        gz, ups, upr, sums, red_c, red_y, red_z,
        load_sem, halo_send, halo_recv, gy_send, gy_recv, gzs_send, gzs_recv,
        u_send, u_recv, rc_send, rc_recv, ry_send, ry_recv, rz_send, rz_recv,
    ) = scratch
    nb = b_hbm.shape[0]
    bs, nr = b_hbm.shape[1:]
    ncb = cb_hbm.shape[0]
    nco = f_hbm.shape[0]
    half = nr // 2
    nrow, ncol = nz * ny, nx * nk
    z, y, x, k = (lax.axis_index(name) for name in ("z", "y", "x", "k"))
    row, col = z * ny + y, x * nk + k
    has_dn, has_up = row > 0, row < nrow - 1

    def row_device(index):
        return {"z": index // ny, "y": lax.rem(index, ny)}

    up_dev = row_device(lax.rem(row + 1, nrow))
    dn_dev = row_device(lax.rem(row + nrow - 1, nrow))

    def col_device(step):
        index = lax.rem(col + step, ncol)
        return {"x": index // nk, "k": lax.rem(index, nk)}

    def y_device(step):
        return {"y": lax.rem(y + step, ny)}

    def z_device(step):
        return {"z": lax.rem(z + step, nz)}

    loads = [
        pltpu.make_async_copy(b_hbm, ev0.at[pl.ds(1, nb)], load_sem.at[0]),
        pltpu.make_async_copy(cb_hbm, cb, load_sem.at[1]),
        pltpu.make_async_copy(lu_hbm, lm.at[pl.ds(0, nb + 1), :, pl.ds(2 * bs, bs)], load_sem.at[2]),
        pltpu.make_async_copy(ld_hbm, lm.at[:, :, pl.ds(bs, bs)], load_sem.at[3]),
        pltpu.make_async_copy(f_hbm, fac, load_sem.at[4]),
        pltpu.make_async_copy(su_hbm, sm.at[:, :, pl.ds(2 * bs, bs)], load_sem.at[5]),
        pltpu.make_async_copy(sd_hbm, sm.at[:, :, pl.ds(bs, bs)], load_sem.at[6]),
    ]
    for load in loads:
        load.start()

    barrier = pltpu.get_barrier_semaphore()
    peers = [up_dev, dn_dev]
    peers += [y_device(s) for s in range(1, ny)]
    peers += [col_device(s) for s in range(1, ncol)]
    peers += [z_device(s) for s in range(1, nz)]
    for peer in peers:
        pl.semaphore_signal(barrier, inc=1, device_id=peer, device_id_type=MESH)

    @pl.when(row == 0)
    def _():
        ev0[0] = jnp.zeros((bs, nr), BF)
        ev1[0] = jnp.zeros((bs, nr), BF)
        yr_dn[...] = jnp.zeros_like(yr_dn)
        tr[...] = jnp.zeros_like(tr)
        cxr_dn[...] = jnp.zeros_like(cxr_dn)
        statr[0] = jnp.zeros(statr.shape[1:], BF)
        usr[0] = jnp.zeros(usr.shape[1:], BF)

    @pl.when(row == nrow - 1)
    def _():
        ev0[nb + 1] = jnp.zeros((bs, nr), BF)
        ev1[nb + 1] = jnp.zeros((bs, nr), BF)
        pv[nb] = jnp.zeros((bs, nr), BF)
        yr_up[...] = jnp.zeros_like(yr_up)
        cxr_up[...] = jnp.zeros_like(cxr_up)
        statr[1] = jnp.zeros(statr.shape[1:], BF)
        usr[1] = jnp.zeros(usr.shape[1:], BF)

    rows_of = lax.broadcasted_iota(jnp.int32, sel.shape, 0)
    slots = lax.broadcasted_iota(jnp.int32, sel.shape, 1)
    slot, j = slots // 8, slots % 8
    owner = jnp.where(slot < nrow, slot * ncol + col, row * ncol + (slot - nrow))
    wanted = jnp.where(j < ncb, owner * ncb + j, -1)
    sel[...] = jnp.where(rows_of == wanted, 1.0, 0.0).astype(BF)

    def lanes(h):
        return pl.ds(h * half, half)

    def to_up(index, src, dst):
        return pltpu.make_async_remote_copy(
            src_ref=src, dst_ref=dst, send_sem=halo_send.at[index], recv_sem=halo_recv.at[index],
            device_id=up_dev, device_id_type=MESH,
        )

    def to_dn(index, src, dst):
        return pltpu.make_async_remote_copy(
            src_ref=src, dst_ref=dst, send_sem=halo_send.at[index], recv_sem=halo_recv.at[index],
            device_id=dn_dev, device_id_type=MESH,
        )

    halo = {}
    for h in range(2):
        at = lanes(h)
        edges = [
            (ev0.at[nb, :, at], ev0.at[0, :, at], ev0.at[1, :, at], ev0.at[nb + 1, :, at]),
            (y_up.at[0, :, at], yr_dn.at[0, :, at], y_dn.at[0, :, at], yr_up.at[0, :, at]),
            (t_up.at[:, at], tr.at[:, at], ed.at[:, at], pv.at[nb, :, at]),
            (ev1.at[nb, :, at], ev1.at[0, :, at], ev1.at[1, :, at], ev1.at[nb + 1, :, at]),
            (y_up.at[1, :, at], yr_dn.at[1, :, at], y_dn.at[1, :, at], yr_up.at[1, :, at]),
        ]
        for phase, (up_src, up_dst, dn_src, dn_dst) in enumerate(edges):
            index = 4 * phase + 2 * h
            halo[phase, h] = (to_up(index, up_src, up_dst), to_dn(index + 1, dn_src, dn_dst))
    halo[5, 0] = (to_up(20, cx, cxr_dn), to_dn(21, ed1, cxr_up))
    halo[6, 0] = (to_up(22, stat.at[0], statr.at[0]), to_dn(23, stat.at[1], statr.at[1]))
    for it in range(2):
        index = 24 + 2 * it
        halo[7 + it, 0] = (
            to_up(index, us.at[it], usr.at[0, it]),
            to_dn(index + 1, us.at[it], usr.at[1, it]),
        )

    def send_up(phase, h):
        pl.when(has_up)(lambda: halo[phase, h][0].start())

    def send_dn(phase, h):
        pl.when(has_dn)(lambda: halo[phase, h][1].start())

    def receive(phase, h):
        pl.when(has_dn)(lambda: halo[phase, h][0].wait_recv())
        pl.when(has_up)(lambda: halo[phase, h][1].wait_recv())

    def y_copies(it):
        here = gz.at[it, z, pl.ds(pl.multiple_of(y * 16, 16), 16)]
        return [
            pltpu.make_async_remote_copy(
                src_ref=here, dst_ref=here, send_sem=gy_send.at[it, s], recv_sem=gy_recv.at[it, s],
                device_id=y_device(s), device_id_type=MESH,
            )
            for s in range(1, ny)
        ]

    def z_copies(it):
        here = gz.at[it, z]
        return [
            pltpu.make_async_remote_copy(
                src_ref=here, dst_ref=here, send_sem=gzs_send.at[it, s], recv_sem=gzs_recv.at[it, s],
                device_id=z_device(s), device_id_type=MESH,
            )
            for s in range(1, nz)
        ]

    def u_copies(it):
        copies = []
        for s in range(1, ncol):
            target = lax.rem(col + s, ncol)
            copies.append(
                pltpu.make_async_remote_copy(
                    src_ref=ups.at[it, target], dst_ref=upr.at[it, s],
                    send_sem=u_send.at[it, s], recv_sem=u_recv.at[it, s],
                    device_id=col_device(s), device_id_type=MESH,
                )
            )
        return copies

    gy = [y_copies(it) for it in range(2)]
    gzc = [z_copies(it) for it in range(2)]
    uc = [u_copies(it) for it in range(2)]

    def coarse_rhs(it, vec):
        g = mm(cb[...], stacked(vec, 1, nb))
        g = jnp.concatenate([g, jnp.zeros((8 - ncb, nr), F32)], axis=0)
        packed = jnp.concatenate([g[:, :half], g[:, half:]], axis=0).astype(BF)
        gz[it, z, pl.ds(pl.multiple_of(y * 16, 16), 16)] = packed

    def coarse_begin(it):
        for copy in gy[it]:
            copy.start()

    def coarse_spread_rows(it):
        for copy in gy[it]:
            copy.wait_recv()
        for copy in gzc[it]:
            copy.start()

    def coarse_solve(it):
        for copy in gzc[it]:
            copy.wait_recv()
        got = gz[it].astype(F32).reshape(nrow, 16, half)
        sides = [got[:, 8 * h : 8 * h + 8].reshape(nrow * 8, half) for h in range(2)]
        g = jnp.concatenate(sides, axis=1).astype(BF)
        u = mm(kk[0], g) + mm(kk[1], g)
        ups[it] = u.reshape(ncol, 8, nr)
        for copy in uc[it]:
            copy.start()

    def coarse_end(it):
        for copy in uc[it]:
            copy.wait_recv()
        u = ups[it, pl.ds(col, 1)].reshape(8, nr)
        for s in range(1, ncol):
            u = u + upr[it, s]
        return u

    def spread(layer, u):
        return lax.dot_general(
            cb[:, pl.ds(pl.multiple_of(layer * bs, bs), bs)], u, (((0,), (0,)), ((), ())),
            preferred_element_type=F32,
        )

    loads[0].wait()
    loads[1].wait()
    coarse_rhs(0, ev0)
    pl.semaphore_wait(barrier, len(peers))
    coarse_begin(0)
    for h in range(2):
        send_up(0, h)
        send_dn(0, h)

    loads[2].wait()

    @pl.loop(0, nb + 1)
    def _(i):
        lm[i + 1, :, pl.ds(0, bs)] = lm[i, :, pl.ds(2 * bs, bs)].T

    coarse_spread_rows(0)

    loads[4].wait()

    @pl.loop(0, nco // 256)
    def _(i):
        at = pl.ds(pl.multiple_of(i * 256, 256), 256)
        fsel[at, :] = mm(fac[at, :], sel[...]).astype(BF)

    split = nrow * 8
    kmat = lax.dot_general(
        fsel[:, split:], fsel[:, :split], (((0,), (0,)), ((), ())), preferred_element_type=F32
    )
    kk[0] = kmat.astype(BF)
    kk[1] = (kmat - kmat.astype(BF).astype(F32)).astype(BF)
    loads[3].wait()

    def half_of(ref, start, count, h):
        return ref[pl.ds(start, count), :, lanes(h)].reshape(count * bs, half)

    def local_middle(vec, out):
        @pl.loop(2, nb)
        def _(i):
            out[i - 1] = mm(lm[i], stacked(vec, i - 1, 3))

    def local_margins(it, vec):
        for h in range(2):
            receive(3 * it, h)
            y_dn[it, :, lanes(h)] = mm(lm[0, :, pl.ds(bs, 2 * bs)], half_of(vec, 0, 2, h)).astype(BF)
            send_dn(3 * it + 1, h)
            y_up[it, :, lanes(h)] = mm(lm[nb + 1, :, pl.ds(0, 2 * bs)], half_of(vec, nb, 2, h)).astype(BF)
            send_up(3 * it + 1, h)

    def local_edges(vec, out):
        @pl.loop(0, 2)
        def _(e):
            i = 1 + e * (nb - 1)
            out[i - 1] = mm(lm[i], stacked(vec, i - 1, 3))

    local_margins(0, ev0)
    local_middle(ev0, q0)
    local_edges(ev0, q0)

    loads[5].wait()

    @pl.loop(0, nb)
    def _(i):
        sut[i] = sm[i, :, pl.ds(2 * bs, bs)].T

    @pl.loop(1, nb)
    def _(i):
        sm[i, :, pl.ds(0, bs)] = sut[i - 1]

    def two_pieces(value):
        top = value.astype(BF).astype(F32)
        return jnp.concatenate([top, value - top], axis=0).astype(BF)

    pad = jnp.zeros((8 - ncb, bs), F32)
    upper = sm[nb - 1, :, pl.ds(2 * bs, bs)]
    stat[0] = two_pieces(jnp.concatenate([mm(cb[:, pl.ds((nb - 1) * bs, bs)], upper), pad], axis=0))
    lowest = cb[:, pl.ds(0, bs)].astype(F32)
    stat[1] = jnp.concatenate([lowest, pad, jnp.zeros((8, bs), F32)], axis=0).astype(BF)
    send_up(6, 0)
    send_dn(6, 0)

    def finish_local(it, out, send):
        for h in range(2):
            at = lanes(h)
            receive(3 * it + 1, h)
            out[0, :, at] += yr_dn[it, :, at].astype(F32)
            out[nb - 1, :, at] += yr_up[it, :, at].astype(F32)
            send(h)

    def finish_coarse(it, out, vec):
        u = coarse_end(it)
        us[it] = jnp.concatenate([u, u], axis=0).astype(BF)
        send_up(7 + it, 0)
        send_dn(7 + it, 0)
        mine = u[:ncb].astype(BF)

        @pl.loop(0, nb)
        def _(i):
            total = out[i] + spread(i, mine)
            out[i] = total
            vec[i] = total.astype(BF)

    def couple(left, u):
        return lax.dot_general(left, u, (((0,), (0,)), ((), ())), preferred_element_type=F32)

    def send_direction(h):
        at = lanes(h)
        ed[:, at] = q0[0, :, at].astype(BF)
        send_dn(2, h)
        t_up[:, at] = mm(sut[nb - 1], q0[nb - 1, :, at].astype(BF)).astype(BF)
        send_up(2, h)

    coarse_solve(0)
    finish_local(0, q0, send_direction)
    loads[6].wait()
    receive(6, 0)
    wup[...] = two_pieces(mm(statr[1], sut[nb - 1])[:8])
    finish_coarse(0, q0, pv)

    def stiff_inside(vec, store):
        store(0, mm(sm[0, :, pl.ds(bs, 2 * bs)], stacked(vec, 0, 2)))
        for i in range(1, nb - 1):
            store(i, mm(sm[i], stacked(vec, i - 1, 3)))
        store(nb - 1, mm(sm[nb - 1, :, pl.ds(0, 2 * bs)], stacked(vec, nb - 2, 2)))

    def store_w0(i, value):
        w0[i] = value

    stiff_inside(pv, store_w0)
    for i in range(1, nb - 1):
        ev1[1 + i] = w0[i].astype(BF)
    for h in range(2):
        at = lanes(h)
        receive(2, h)
        ub[:, at] = mm(sm[nb - 1, :, pl.ds(2 * bs, bs)], pv[nb, :, at])
        if h == 0:
            receive(7, 0)
        ub[:, at] += couple(wup[...], usr[1, 0, :, at])
        trf[:, at] = tr[:, at].astype(F32) + couple(statr[0], usr[0, 0, :, at])
        low = w0[0, :, at] + trf[:, at]
        high = w0[nb - 1, :, at] + ub[:, at]
        w0[0, :, at] = low
        w0[nb - 1, :, at] = high
        ev1[1, :, at] = low.astype(BF)
        ev1[nb, :, at] = high.astype(BF)
        if h == 1:
            coarse_rhs(1, ev1)
            coarse_begin(1)
        send_dn(3, h)
        send_up(3, h)

    def columns(value):
        return jnp.sum(value, axis=0, keepdims=True)

    s1 = jnp.zeros((1, nr), F32)
    s2 = jnp.zeros((1, nr), F32)
    for i in range(nb):
        s1 = s1 + columns(ev0[1 + i].astype(F32) * q0[i])
        s2 = s2 + columns(w0[i] * q0[i])

    local_middle(ev1, q1)
    coarse_spread_rows(1)
    local_margins(1, ev1)
    local_edges(ev1, q1)
    coarse_solve(1)

    def send_cross(h):
        if h == 0:
            ed1[...] = q1[0, :, lanes(0)].astype(BF)
            send_dn(5, 0)
        else:
            cx[...] = mm(sut[nb - 1], q1[nb - 1, :, lanes(1)].astype(BF)).astype(BF)
            send_up(5, 0)

    finish_local(1, q1, send_cross)
    finish_coarse(1, q1, pv1)

    s3 = jnp.zeros((1, nr), F32)
    s4 = jnp.zeros((1, nr), F32)
    for i in range(nb):
        s3 = s3 + columns(ev0[1 + i].astype(F32) * q1[i])
        s4 = s4 + columns(w0[i] * q1[i])
    s5 = columns(trf[...] * q1[0]) + columns(ub[...] * q1[nb - 1])
    mixed = []

    def add_dots(i, value):
        mixed.append((columns(q0[i] * value), columns(q1[i] * value)))

    stiff_inside(pv1, add_dots)
    s5 = s5 + sum(pair[0] for pair in mixed)
    s6 = sum(pair[1] for pair in mixed)
    receive(5, 0)
    from_up = mm(sm[nb - 1, :, pl.ds(2 * bs, bs)], cxr_up[...])
    receive(8, 0)
    from_up = from_up + couple(wup[...], usr[1, 1, :, lanes(0)])
    from_dn = cxr_dn[...].astype(F32) + couple(statr[0], usr[0, 1, :, lanes(1)])
    cross_up = columns(from_up * q1[nb - 1, :, pl.ds(0, half)])
    cross_dn = columns(from_dn * q1[0, :, pl.ds(half, half)])
    s6 = s6 + 2.0 * jnp.concatenate([cross_up, cross_dn], axis=1)

    sums[0] = jnp.concatenate([s1, s2, s3, s4, s5, s6, jnp.zeros((2, nr), F32)], axis=0)

    def reduce_stage(stage, buf, device, count, send, recv):
        copies = [
            pltpu.make_async_remote_copy(
                src_ref=sums.at[stage], dst_ref=buf.at[s], send_sem=send.at[s], recv_sem=recv.at[s],
                device_id=device(s), device_id_type=MESH,
            )
            for s in range(1, count)
        ]
        for copy in copies:
            copy.start()
        total = sums[stage]
        for s, copy in enumerate(copies, 1):
            copy.wait_recv()
            total = total + buf[s]
        return copies, total

    sent_c, total = reduce_stage(0, red_c, col_device, ncol, rc_send, rc_recv)
    sums[1] = total
    sent_y, total = reduce_stage(1, red_y, y_device, ny, ry_send, ry_recv)
    sums[2] = total
    sent_z, total = reduce_stage(2, red_z, z_device, nz, rz_send, rz_recv)

    d = [total[i : i + 1] for i in range(6)]
    alpha = d[0] / d[1]
    rho = d[0] - alpha * (d[2] + d[1]) + alpha * alpha * d[3]
    grow = 1.0 + rho / d[0]
    denom = grow * grow * d[1] - grow * alpha * (d[4] + d[3]) + alpha * alpha * d[5]
    step = rho / denom
    c0 = jnp.broadcast_to(alpha + step * grow, (bs, nr))
    c1 = jnp.broadcast_to(alpha * step, (bs, nr))
    for i in range(nb):
        x_ref[i] = c0 * q0[i] - c1 * q1[i]

    for copy in sent_c + sent_y + sent_z + gy[0] + gy[1] + gzc[0] + gzc[1] + uc[0] + uc[1]:
        copy.wait_send()
    for up, dn in halo.values():
        pl.when(has_up)(lambda up=up: up.wait_send())
        pl.when(has_dn)(lambda dn=dn: dn.wait_send())


def on_device(sizes, b, sd, su, ld, lu, cb, fac):
    nz, ny, nx, nk = sizes
    b, sd, su, ld, lu = (a[:, 0] for a in (b, sd, su, ld, lu))
    cb = cb[0, 0]
    nb, bs, nr = b.shape
    ncb = cb.shape[0]
    nco = fac.shape[0]
    nrow, ncol = nz * ny, nx * nk
    half = nr // 2
    nsel = 8 * (nrow + ncol)
    dma = pltpu.SemaphoreType.DMA
    vm = pltpu.VMEM
    scratch = [
        vm((nb + 2, bs, 3 * bs), BF),
        vm((nb, bs, 3 * bs), BF),
        vm((nb, bs, bs), BF),
        vm((ncb, nb * bs), BF),
        vm((nco, nco), BF),
        vm((nco, nsel), BF),
        vm((nco, nsel), BF),
        vm((2, 8 * ncol, 8 * nrow), BF),
        vm((nb + 2, bs, nr), BF),
        vm((nb + 2, bs, nr), BF),
        vm((nb + 1, bs, nr), BF),
        vm((nb, bs, nr), BF),
        vm((nb, bs, nr), F32),
        vm((nb, bs, nr), F32),
        vm((nb, bs, nr), F32),
        vm((2, bs, nr), BF),
        vm((2, bs, nr), BF),
        vm((2, bs, nr), BF),
        vm((2, bs, nr), BF),
        vm((bs, nr), BF),
        vm((bs, nr), BF),
        vm((bs, nr), F32),
        vm((bs, nr), F32),
        vm((bs, half), BF),
        vm((bs, half), BF),
        vm((bs, half), BF),
        vm((bs, nr), BF),
        vm((bs, half), BF),
        vm((2, 16, bs), BF),
        vm((2, 16, bs), BF),
        vm((16, bs), BF),
        vm((2, 16, nr), BF),
        vm((2, 2, 16, nr), BF),
        vm((2, nz, ny * 16, half), BF),
        vm((2, ncol, 8, nr), F32),
        vm((2, ncol, 8, nr), F32),
        vm((3, 8, nr), F32),
        vm((ncol, 8, nr), F32),
        vm((ny, 8, nr), F32),
        vm((nz, 8, nr), F32),
        dma((7,)),
        dma((28,)),
        dma((28,)),
        dma((2, ny)),
        dma((2, ny)),
        dma((2, nz)),
        dma((2, nz)),
        dma((2, ncol)),
        dma((2, ncol)),
        dma((ncol,)),
        dma((ncol,)),
        dma((ny,)),
        dma((ny,)),
        dma((nz,)),
        dma((nz,)),
    ]
    out = pl.pallas_call(
        functools.partial(kernel, sizes),
        out_shape=jax.ShapeDtypeStruct((nb, bs, nr), F32),
        in_specs=[pl.BlockSpec(memory_space=pl.ANY)] * 7,
        out_specs=pl.BlockSpec(memory_space=pltpu.VMEM),
        scratch_shapes=scratch,
        compiler_params=pltpu.CompilerParams(
            collective_id=0, has_side_effects=True, vmem_limit_bytes=60 * 1024 * 1024
        ),
        name="schwarz_pcg",
    )(b, sd, su, ld, lu, cb, fac)
    return out[:, None]


def solution(mesh):
    sizes = (8, 4, 4, 2)
    if mesh.devices.size != 256:
        sizes = (2, 2, 2, 2)
    split = Mesh(mesh.devices.reshape(sizes), ("z", "y", "x", "k"))
    row, col = ("z", "y"), ("x", "k")
    spec = P(row, col, None, None)
    return jax.shard_map(
        functools.partial(on_device, sizes),
        mesh=split,
        in_specs=(spec,) * 6 + (P(),),
        out_specs=spec,
        check_vma=False,
    )
```
